256 devices in a mesh: tile: 32 (over x, z), lev: 8 (over y, core).
Axes of the slice: x: 4, y: 4, z: 8, core: 2. Of those that a mesh axis runs over, the one named last changes fastest.
Arguments:
- ocean_state: bfloat16 [8, 512, 1024, 128], P('lev', 'tile'), may hold values from -6 to 6
- tile_owner: int32 [32, 64], replicated, may hold values from -1 to 1023, as said below
- kernel: bfloat16 [7, 7, 128], replicated, may hold values from -0.875 to 0.875
- bias_dw: float32 [128], replicated, may hold values from -3 to 3
- ln_gain: float32 [128], replicated, may hold values from 0.5 to 2
- ln_bias: float32 [128], replicated, may hold values from -3 to 3
- w_in: bfloat16 [128, 512], replicated, may hold values from -0.5 to 0.5
- b_in: float32 [512], replicated, may hold values from -3 to 3
- w_out: bfloat16 [512, 128], replicated, may hold values from -0.25 to 0.25
- b_out: float32 [128], replicated, may hold values from -3 to 3
- layer_scale: float32 [128], replicated, may hold values from 0.3 to 1.5
- w_vert: bfloat16 [5, 128, 128], replicated, may hold values from -0.25 to 0.25
Outputs:
- updated: bfloat16 [1024, 8, 256, 128], P('tile', None, 'lev')
The draws below stay inside these ranges and needn't reach their ends.
Inputs may be any that keep to these rules, and one draw needn't show every extreme that they name: `tile_owner`: every value from 0 to 1023 appears exactly once; -1 marks a land tile. Value g names owner g // 32, so every owner receives exactly 32 tiles. No latitude row sends more than 2 tiles to one owner, and in every draw some row sends exactly 2 to some owner.
All inputs are finite; a program needn't handle non-finite values.
Results may differ from the reference program's by a relative error of at most 0.006.
Values may be sent and summed in bfloat16 or wider, within the bound.
No kernel may reach another device: no remote copies, remote signals or barrier semaphores. Data moves between devices by JAX's collectives and lax.ppermute only.
A program may use at most 64 MiB of HBM per device.

```python
import math
import jax
import jax.numpy as jnp
from jax import lax

C = 128
HID = 512
TS = 16
KS = 7
VK = 5
CAP = 2
LEVELS = 8
NLAT = 32
NLON = 64
OWN = 32
WET = 1024


def draw_tile_owner(key, part):
    band_count = NLAT
    keys = jax.random.split(key, 4)
    quarter = max(band_count // 4, 1)
    base_tilt = jnp.concatenate([jnp.ones((quarter,), jnp.int32), -jnp.ones((quarter,), jnp.int32), jnp.zeros((band_count - 2 * quarter,), jnp.int32)])
    tilt = jax.random.permutation(keys[0], base_tilt)
    lifted = jax.random.randint(keys[1], (band_count,), 0, 2).astype(jnp.int32)
    chosen = jax.random.randint(keys[2], (), 0, band_count)
    lifted = jnp.where(jnp.arange(band_count) == chosen, 1, lifted).astype(jnp.int32)
    pair_count = 1 + tilt[:, None] * lifted[None, :]
    first_slot = jnp.cumsum(pair_count, axis=0) - pair_count
    entry_dest = jnp.repeat(jnp.arange(band_count, dtype=jnp.int32), CAP)
    entry_rank = jnp.tile(jnp.arange(CAP, dtype=jnp.int32), band_count)
    valid = entry_rank[None, :] < pair_count[:, entry_dest]
    value = entry_dest[None, :] * OWN + first_slot[:, entry_dest] + entry_rank[None, :]
    order_key = jnp.where(valid, 0, 1).astype(jnp.int32)
    arranged_order = jnp.argsort(order_key, axis=1, stable=True)
    arranged = jnp.take_along_axis(jnp.where(valid, value, -1), arranged_order, axis=1)
    row_keys = jax.random.split(keys[3], band_count)
    places = jax.vmap(lambda row_key: jax.random.permutation(row_key, NLON))(row_keys)
    inverse = jnp.argsort(places, axis=1)
    return jnp.take_along_axis(arranged, inverse, axis=1).astype(jnp.int32)


def steps_of(stream_key, extent, cuts, least, high):
    level, own = 1.0, jax.random.fold_in(stream_key, 6)
    for position, parts in cuts:
        steps = jnp.exp(jax.random.uniform(jax.random.fold_in(own, position), (parts,), jnp.float32, least / len(cuts), high / len(cuts)))
        level = level * jnp.repeat(steps, extent[position] // parts).reshape([-1 if axis == position else 1 for axis in range(len(extent))])
    return level


def scatter_about(key, dims, deviation, bound, shards=(), held_as=jnp.bfloat16):
    gain = steps_of(key, dims, shards, -0.22, 0.18) if shards else 1.0
    entries = jax.random.normal(key, dims, jnp.float32) * deviation * gain
    return jnp.minimum(jnp.maximum(entries, -bound), bound).astype(held_as)


def setup_inputs(seed: int = 0) -> dict:
    key_list = jax.random.split(jax.random.key(seed), 13)
    ocean_state = scatter_about(key_list[0], (LEVELS, NLAT * TS, NLON * TS, C), 1.0, 6.0, ((0, 8), (1, 32)))
    tile_owner = draw_tile_owner(jax.random.fold_in(key_list[12], 71), 0)
    kernel = scatter_about(key_list[2], (KS, KS, C), (KS * KS) ** -0.5, 0.875)
    bias_dw = scatter_about(key_list[3], (C,), 0.5, 3.0, (), jnp.float32)
    ln_gain = jnp.clip(jnp.exp(jax.random.uniform(key_list[4], (C,), jnp.float32, math.log(0.5), math.log(2.0))), 0.5, 2.0)
    ln_bias = scatter_about(key_list[5], (C,), 0.5, 3.0, (), jnp.float32)
    w_in = scatter_about(key_list[6], (C, HID), C ** -0.5, 0.5)
    b_in = scatter_about(key_list[7], (HID,), 0.5, 3.0, (), jnp.float32)
    w_out = scatter_about(key_list[8], (HID, C), HID ** -0.5, 0.25)
    b_out = scatter_about(key_list[9], (C,), 0.5, 3.0, (), jnp.float32)
    layer_scale = jnp.clip(jnp.exp(jax.random.uniform(key_list[10], (C,), jnp.float32, math.log(0.3), math.log(1.5))), 0.3, 1.5)
    w_vert = scatter_about(key_list[11], (VK, C, C), (VK * C) ** -0.5, 0.25)
    return dict(ocean_state=ocean_state, tile_owner=tile_owner, kernel=kernel, bias_dw=bias_dw, ln_gain=ln_gain, ln_bias=ln_bias, w_in=w_in, b_in=b_in, w_out=w_out, b_out=b_out, layer_scale=layer_scale, w_vert=w_vert)


def depthwise(padded, kernel, bias_dw, rows, cols):
    total = jnp.zeros(padded.shape[:-3] + (rows, cols, padded.shape[-1]), jnp.float32) + bias_dw.astype(jnp.float32)
    for i in range(7):
        for j in range(7):
            total = total + padded[..., i:i + rows, j:j + cols, :].astype(jnp.float32) * kernel[i, j].astype(jnp.float32)
    return total.astype(jnp.bfloat16)

def feed_forward(conv_rows, input_rows, ln_gain, ln_bias, w_in, b_in, w_out, b_out, layer_scale):
    values = conv_rows.astype(jnp.float32)
    centre = lax.optimization_barrier(jnp.mean(values, axis=-1, keepdims=True))
    spread = lax.optimization_barrier(jnp.mean((values - centre) ** 2, axis=-1, keepdims=True))
    normed = ((values - centre) / jnp.sqrt(spread + 1e-06) * ln_gain + ln_bias).astype(jnp.bfloat16)
    hidden = jax.nn.gelu(jnp.dot(normed, w_in, preferred_element_type=jnp.float32) + b_in, approximate=False).astype(jnp.bfloat16)
    branch = jnp.dot(hidden, w_out, preferred_element_type=jnp.float32) + b_out
    return (input_rows.astype(jnp.float32) + layer_scale * branch).astype(jnp.bfloat16)

def vertical(block_mid, w_vert):
    level_count = block_mid.shape[-3]
    widths = [(0, 0)] * (block_mid.ndim - 3) + [(2, 2), (0, 0), (0, 0)]
    level_pad = jnp.pad(block_mid, widths)
    channels = block_mid.shape[-1]
    total = block_mid.astype(jnp.float32)
    for k in range(5):
        taken = level_pad[..., k:k + level_count, :, :].reshape(-1, channels)
        total = total + jnp.dot(taken, w_vert[k], preferred_element_type=jnp.float32).reshape(block_mid.shape)
    return total.astype(jnp.bfloat16)

def reference(ocean_state, tile_owner, kernel, bias_dw, ln_gain, ln_bias, w_in, b_in, w_out, b_out, layer_scale, w_vert):
    wet_cells = jnp.repeat(jnp.repeat(tile_owner >= 0, TS, axis=0), TS, axis=1)
    masked = jnp.where(wet_cells[None, :, :, None], ocean_state, jnp.zeros((), jnp.bfloat16))

    def one_level(level):
        padded = jnp.pad(level, ((3, 3), (0, 0), (0, 0)))
        padded = jnp.concatenate([padded[:, -3:], padded, padded[:, :3]], axis=1)
        return depthwise(padded, kernel, bias_dw, NLAT * TS, NLON * TS)
    conv_out = lax.map(one_level, masked)

    def to_tiles(field_in):
        shaped = field_in.reshape(LEVELS, NLAT, TS, NLON, TS, C).transpose(1, 3, 0, 2, 4, 5)
        return shaped.reshape(NLAT * NLON, LEVELS, TS * TS, C)
    owner_flat = tile_owner.reshape(-1)
    slot_index = jnp.where(owner_flat >= 0, owner_flat, WET).astype(jnp.int32)
    order_index = jnp.zeros((WET,), jnp.int32).at[slot_index].set(jnp.arange(NLAT * NLON, dtype=jnp.int32), mode='drop')
    tile_conv = to_tiles(conv_out)[order_index]
    tile_input = to_tiles(masked)[order_index]

    def apply_tile(blocks):
        conv_rows = blocks[0].reshape(-1, C)
        input_rows = blocks[1].reshape(-1, C)
        block_mid = feed_forward(conv_rows, input_rows, ln_gain, ln_bias, w_in, b_in, w_out, b_out, layer_scale)
        return vertical(block_mid.reshape(LEVELS, TS * TS, C), w_vert)
    return lax.map(apply_tile, (tile_conv, tile_input))
```

```python
import functools

import jax
import jax.numpy as jnp
from jax import lax
from jax.experimental import pallas as pl
from jax.experimental.pallas import tpu as pltpu
from jax.sharding import PartitionSpec as P

CAP = 2
TS = 16
C = 128
F32 = jnp.float32
BF16 = jnp.bfloat16
SLOTS = 2


def list_wet(owner_ref, band, seen, cols, slots):
    lon = owner_ref.shape[1]
    per_owner = owner_ref.shape[0]

    def clear(o, _):
        seen[o] = 0
        return 0

    lax.fori_loop(0, per_owner, clear, 0)

    def scan(c, count):
        g = owner_ref[band, c]
        wet = g >= 0
        dest = lax.shift_right_logical(jnp.maximum(g, 0), per_owner.bit_length() - 1)
        rank = seen[dest]
        cols[count] = c
        slots[count] = dest * CAP + rank
        seen[dest] = rank + wet.astype(jnp.int32)
        return count + wet.astype(jnp.int32)

    return lax.fori_loop(0, lon, scan, 0)


def conv_rows(pad_ref, first, taps, bias, rows):
    total = [[bias, bias] for _ in range(rows)]
    for j in range(7):
        ks = [taps[i * 7 + j] for i in range(7)]
        for yi in range(rows + 6):
            for h in range(2):
                v = pad_ref[first + yi, pl.ds(5 + j + 8 * h, 8), :]
                for i in range(7):
                    y = yi - i
                    if 0 <= y < rows:
                        total[y][h] = total[y][h] + v * ks[i]
    return jnp.concatenate([t for pair in total for t in pair], axis=0)


def pointwise(conv, inp, gain, shift, w_in, b_in, w_out, b_out, scale):
    values = conv.astype(F32)
    centre = jnp.mean(values, axis=-1, keepdims=True)
    dev = values - centre
    spread = jnp.mean(dev * dev, axis=-1, keepdims=True)
    normed = (dev * lax.rsqrt(spread + 1e-06) * gain + shift).astype(BF16)
    h = jnp.dot(normed, w_in, preferred_element_type=F32) + b_in
    half = 0.5 * h
    hidden = (half + half * lax.erf(h * 0.7071067811865476)).astype(BF16)
    branch = jnp.dot(hidden, w_out, preferred_element_type=F32) + b_out
    return (inp.astype(F32) + scale * branch).astype(BF16)


def fill(pad_ref, first, src, row0, rows, t, lon, wet):
    left = lax.rem(t + lon - 1, lon)
    right = lax.rem(t + 1, lon)

    def tile(col):
        return src[pl.ds(row0, rows), pl.ds(pl.multiple_of(col * TS, TS), TS), :].astype(F32)

    keep_l, keep_c, keep_r = wet
    zero = jnp.zeros((), F32)
    centre = tile(t)
    if keep_c is not None:
        centre = jnp.where(keep_c, centre, zero)
    pad_ref[pl.ds(first, rows), pl.ds(0, 8), :] = jnp.where(keep_l, tile(left)[:, 8:, :], zero)
    pad_ref[pl.ds(first, rows), pl.ds(8, 16), :] = centre
    pad_ref[pl.ds(first, rows), pl.ds(24, 8), :] = jnp.where(keep_r, tile(right)[:, :8, :], zero)


def neighbours(owner_ref, band, t, lon):
    left = lax.rem(t + lon - 1, lon)
    right = lax.rem(t + 1, lon)
    return (owner_ref[band, left] >= 0, owner_ref[band, t] >= 0, owner_ref[band, right] >= 0)


def block_kernel(inner, *refs):
    if inner:
        (owner_ref, x_ref, taps_in, bias_ref, gain, shift, w_in, b_in, w_out, b_out, scale,
         send, pad, taps, convbuf, stage, seen, cols, slots, sem) = refs
        top = bottom = None
    else:
        (owner_ref, x_ref, top, bottom, taps_in, bias_ref, gain, shift, w_in, b_in, w_out, b_out,
         scale, _, send, pad, taps, convbuf, stage, seen, cols, slots, sem) = refs
    lon = owner_ref.shape[1]
    bands = owner_ref.shape[0]
    band = lax.axis_index("tile")
    count = list_wet(owner_ref, band, seen, cols, slots)
    for i in range(7):
        for j in range(7):
            taps[i * 7 + j] = jnp.broadcast_to(taps_in[i, pl.ds(j, 1), :].astype(F32), (8, C))
    convbuf[...] = jnp.zeros_like(convbuf)
    cells = convbuf.shape[0]

    def copies(index, b):
        slot = slots[index]
        dest, rank = lax.shift_right_logical(slot, 1), lax.bitwise_and(slot, 1)

        def piece(q, lo, n, lev, nlev, off, width):
            if nlev > 1:
                src = stage.at[b, pl.ds(lo, n)].reshape(nlev, width, C)
                dst = send.at[dest, pl.ds(lev, nlev), rank]
            else:
                src = stage.at[b, pl.ds(lo, n)]
                dst = send.at[dest, lev, rank, pl.ds(off, width)]
            return pltpu.make_async_copy(src, dst, sem.at[b, q])

        if inner:
            return [piece(0, 0, 16, 1, 1, 16, 16), piece(1, 16, 128, 2, 4, 0, 32),
                    piece(2, 144, 16, 6, 1, 0, 16)]
        return [piece(0, 0, 32, 0, 1, 0, 32), piece(1, 32, 16, 1, 1, 0, 16),
                piece(2, 48, 16, 6, 1, 16, 16), piece(3, 64, 32, 7, 1, 0, 32)]

    def step(n, _):
        now = jnp.minimum(n, count - 1)
        before = jnp.maximum(n - 1, 0)
        b = lax.rem(before, SLOTS)

        @pl.when(n > SLOTS)
        def _():
            for cp in copies(before - SLOTS, b):
                cp.wait()

        t, tb = cols[now], cols[before]
        own = neighbours(owner_ref, band, t, lon)
        old = convbuf[...]
        column = pl.ds(pl.multiple_of(tb * TS, TS), TS)
        if inner:
            inp = x_ref[pl.ds(3, 10), column, :].reshape(cells, C)
        else:
            inp = jnp.concatenate(
                [x_ref[pl.ds(0, 3), column, :].reshape(cells // 2, C),
                 x_ref[pl.ds(13, 3), column, :].reshape(cells // 2, C)], axis=0)
        stage[b] = pointwise(old, inp, gain[...], shift[...], w_in[...], b_in[...], w_out[...],
                             b_out[...], scale[...])
        bias = jnp.broadcast_to(bias_ref[...], (8, C))
        keep = (own[0], None, own[2])
        if inner:
            fill(pad, 0, x_ref, 0, 16, t, lon, keep)
            convbuf[...] = conv_rows(pad, 0, taps, bias, 10).astype(BF16)
        else:
            up = neighbours(owner_ref, jnp.maximum(band - 1, 0), t, lon)
            down = neighbours(owner_ref, jnp.minimum(band + 1, bands - 1), t, lon)
            fill(pad, 0, top, 0, 3, t, lon, up)
            fill(pad, 3, x_ref, 0, 6, t, lon, keep)
            fill(pad, 9, x_ref, 10, 6, t, lon, keep)
            fill(pad, 15, bottom, 0, 3, t, lon, down)
            convbuf[pl.ds(0, 48)] = conv_rows(pad, 0, taps, bias, 3).astype(BF16)
            convbuf[pl.ds(48, 48)] = conv_rows(pad, 9, taps, bias, 3).astype(BF16)

        @pl.when(n > 0)
        def _():
            for cp in copies(before, b):
                cp.start()

        return 0

    @pl.when(count > 0)
    def _():
        lax.fori_loop(0, count + 1, step, 0)
        for d in range(SLOTS, 0, -1):
            @pl.when(count >= d)
            def _():
                for cp in copies(count - d, lax.rem(count - d, SLOTS)):
                    cp.wait()


def block_call(inner, owner, x, halos, consts, sent, levels):
    bands, lon = owner.shape
    vmem = pl.BlockSpec(memory_space=pltpu.VMEM)
    smem = pl.BlockSpec(memory_space=pltpu.SMEM)
    hbm = pl.BlockSpec(memory_space=pltpu.HBM)
    args = [owner, x, *halos, *consts]
    specs = [smem] + [vmem] * (len(args) - 1)
    aliases = {}
    if sent is not None:
        aliases = {len(args): 0}
        args.append(sent)
        specs.append(hbm)
    cells = 160 if inner else 96
    return pl.pallas_call(
        functools.partial(block_kernel, inner),
        in_specs=specs,
        out_specs=hbm,
        out_shape=jax.ShapeDtypeStruct((bands, levels, CAP, TS * TS // levels, C), BF16),
        scratch_shapes=[
            pltpu.VMEM((16 if inner else 18, 32, C), F32),
            pltpu.VMEM((49, 8, C), F32),
            pltpu.VMEM((cells, C), BF16),
            pltpu.VMEM((SLOTS, cells, C), BF16),
            pltpu.SMEM((bands,), jnp.int32),
            pltpu.SMEM((lon + 1,), jnp.int32),
            pltpu.SMEM((lon + 1,), jnp.int32),
            pltpu.SemaphoreType.DMA((SLOTS, 4)),
        ],
        input_output_aliases=aliases,
        compiler_params=pltpu.CompilerParams(vmem_limit_bytes=32 << 20),
        name="inner_rows" if inner else "edge_rows",
    )(*args)


def vertical_kernel(src, rank, recv, w, out, held, done, sem_in, sem_out):
    tiles = held.shape[0]
    levels, cells = held.shape[1], held.shape[2]

    def fetch(t):
        return pltpu.make_async_copy(recv.at[src[t], :, rank[t]], held.at[t], sem_in.at[t])

    def store(t):
        return pltpu.make_async_copy(done.at[t], out.at[t], sem_out.at[t])

    def start(t, _):
        fetch(t).start()
        return 0

    lax.fori_loop(0, tiles, start, 0)

    def step(t, _):
        fetch(t).wait()
        x = held[t].reshape(levels * cells, C)
        zero = jnp.zeros((2 * cells, C), BF16)
        padded = jnp.concatenate([zero, x, zero], axis=0)
        wide = jnp.concatenate(
            [padded[k * cells : (k + levels) * cells] for k in range(5)], axis=1)
        total = x.astype(F32) + jnp.dot(wide, w[...], preferred_element_type=F32)
        done[t] = total.astype(BF16).reshape(levels, cells, C)
        store(t).start()
        return 0

    lax.fori_loop(0, tiles, step, 0)

    def drain(t, _):
        store(t).wait()
        return 0

    lax.fori_loop(0, tiles, drain, 0)


def vertical_call(src, rank, recv, w_vert):
    tiles = src.shape[0]
    levels, cells = recv.shape[1], recv.shape[3]
    smem = pl.BlockSpec(memory_space=pltpu.SMEM)
    hbm = pl.BlockSpec(memory_space=pltpu.HBM)
    return pl.pallas_call(
        vertical_kernel,
        in_specs=[smem, smem, hbm, pl.BlockSpec(memory_space=pltpu.VMEM)],
        out_specs=hbm,
        out_shape=jax.ShapeDtypeStruct((tiles, levels, cells, C), BF16),
        scratch_shapes=[
            pltpu.VMEM((tiles, levels, cells, C), BF16),
            pltpu.VMEM((tiles, levels, cells, C), BF16),
            pltpu.SemaphoreType.DMA((tiles,)),
            pltpu.SemaphoreType.DMA((tiles,)),
        ],
        compiler_params=pltpu.CompilerParams(vmem_limit_bytes=32 << 20),
        name="vertical",
    )(src, rank, recv, w_vert.reshape(5 * C, C))


def body(ocean_state, tile_owner, kernel, bias_dw, ln_gain, ln_bias, w_in, b_in, w_out, b_out,
         layer_scale, w_vert):
    bands, lon = tile_owner.shape
    levels = lax.axis_size("lev")
    band = lax.axis_index("tile")
    x = ocean_state[0]
    ends = bands - 1
    top = lax.ppermute(x[TS - 3 :], "tile", [(i, i + 1) for i in range(ends)])
    bottom = lax.ppermute(x[:3], "tile", [(i + 1, i) for i in range(ends)])
    row = lambda v: v.reshape(1, -1)
    consts = (kernel, row(bias_dw), row(ln_gain), row(ln_bias), w_in, row(b_in), w_out, row(b_out),
              row(layer_scale))
    sent = block_call(True, tile_owner, x, (), consts, None, levels)
    sent = block_call(False, tile_owner, x, (top, bottom), consts, sent, levels)
    cells = TS * TS // levels
    received = lax.all_to_all(
        sent.reshape(bands * levels, CAP * cells, C), ("tile", "lev"), split_axis=0,
        concat_axis=0, tiled=True,
    ).reshape(bands, levels, CAP, cells, C)

    owner_of = jnp.where(tile_owner >= 0, tile_owner // bands, -1)
    mine = owner_of == band
    before = jnp.cumsum(mine.astype(jnp.int32), axis=1) - mine
    hit = (tile_owner.reshape(1, -1) == (band * bands + jnp.arange(bands))[:, None])
    code = jnp.arange(bands, dtype=jnp.int32)[:, None] * CAP + before
    found = jnp.sum(jnp.where(hit, code.reshape(1, -1), 0), axis=1)
    return vertical_call(found // CAP, found % CAP, received, w_vert)


def solution(mesh):
    return jax.shard_map(
        body,
        mesh=mesh,
        in_specs=(P("lev", "tile", None, None),) + (P(),) * 11,
        out_specs=P("tile", None, "lev", None),
        check_vma=False,
    )
```

```python
import functools

import jax
import jax.numpy as jnp
from jax import lax
from jax.experimental import pallas as pl
from jax.experimental.pallas import tpu as pltpu
from jax.sharding import PartitionSpec as P

CAP = 2
TS = 16
C = 128
F32 = jnp.float32
BF16 = jnp.bfloat16
SLOTS = 2
VMEM_BYTES = 63 << 20


def list_wet(owner_ref, band, want, seen, cols, dests):
    bands, lon = owner_ref.shape

    def clear(o, _):
        seen[o] = 0
        return 0

    lax.fori_loop(0, bands, clear, 0)

    def scan(c, count):
        g = owner_ref[band, c]
        dest = lax.shift_right_logical(jnp.maximum(g, 0), bands.bit_length() - 1)
        rank = seen[dest]
        cols[count] = c
        dests[count] = dest
        seen[dest] = rank + (g >= 0).astype(jnp.int32)
        return count + ((g >= 0) & (rank == want)).astype(jnp.int32)

    return lax.fori_loop(0, lon, scan, 0)


def conv_rows(pad_ref, first, taps, bias, rows):
    total = [[bias, bias] for _ in range(rows)]
    for j in range(7):
        ks = [taps[i * 7 + j] for i in range(7)]
        for yi in range(rows + 6):
            for h in range(2):
                v = pad_ref[first + yi, pl.ds(5 + j + 8 * h, 8), :]
                for i in range(7):
                    y = yi - i
                    if 0 <= y < rows:
                        total[y][h] = total[y][h] + v * ks[i]
    return jnp.concatenate([t for pair in total for t in pair], axis=0)


def pointwise(conv, inp, gain, shift, w_in, b_in, w_out, b_out, scale):
    values = conv.astype(F32)
    centre = jnp.mean(values, axis=-1, keepdims=True)
    dev = values - centre
    spread = jnp.mean(dev * dev, axis=-1, keepdims=True)
    normed = (dev * lax.rsqrt(spread + 1e-06) * gain + shift).astype(BF16)
    h = jnp.dot(normed, w_in, preferred_element_type=F32) + b_in
    half = 0.5 * h
    hidden = (half + half * lax.erf(h * 0.7071067811865476)).astype(BF16)
    branch = jnp.dot(hidden, w_out, preferred_element_type=F32) + b_out
    return (inp.astype(F32) + scale * branch).astype(BF16)


def fill(pad_ref, first, src, row0, rows, t, lon, wet):
    left = lax.rem(t + lon - 1, lon)
    right = lax.rem(t + 1, lon)

    def tile(col):
        return src[pl.ds(row0, rows), pl.ds(pl.multiple_of(col * TS, TS), TS), :].astype(F32)

    keep_l, keep_c, keep_r = wet
    zero = jnp.zeros((), F32)
    centre = tile(t)
    if keep_c is not None:
        centre = jnp.where(keep_c, centre, zero)
    pad_ref[pl.ds(first, rows), pl.ds(0, 8), :] = jnp.where(keep_l, tile(left)[:, 8:, :], zero)
    pad_ref[pl.ds(first, rows), pl.ds(8, 16), :] = centre
    pad_ref[pl.ds(first, rows), pl.ds(24, 8), :] = jnp.where(keep_r, tile(right)[:, :8, :], zero)


def neighbours(owner_ref, band, t, lon):
    left = lax.rem(t + lon - 1, lon)
    right = lax.rem(t + 1, lon)
    return (owner_ref[band, left] >= 0, owner_ref[band, t] >= 0, owner_ref[band, right] >= 0)


INNER, EDGES, FULL = "inner_rows", "edge_rows", "full_rows"
CELLS = {INNER: 160, EDGES: 96, FULL: 256}


def block_kernel(rows, want, batch, n_args, n_pass, *refs):
    args, refs = refs[:n_args], refs[n_args + n_pass :]
    send, refs = refs[0], refs[1:]
    held, refs = refs[:n_args], refs[n_args:]
    pad, taps, convbuf, inbuf, stage, seen, cols, dests, sem, load = refs
    loads = []
    for q, (src, dst) in enumerate(zip(args, held)):
        if rows == EDGES and q == 1:
            loads.append(pltpu.make_async_copy(src.at[pl.ds(0, 6)], dst.at[pl.ds(0, 6)], load.at[q]))
            loads.append(pltpu.make_async_copy(src.at[pl.ds(10, 6)], dst.at[pl.ds(6, 6)], load.at[n_args]))
        else:
            loads.append(pltpu.make_async_copy(src, dst, load.at[q]))
    for cp in loads:
        cp.start()
    for cp in loads:
        cp.wait()
    owner_ref, x_ref = held[:2]
    if rows != INNER:
        top, bottom = held[2:4]
    taps_in, bias_ref, gain, shift, w_in, b_in, w_out, b_out, scale = held[-9:]
    bands, lon = owner_ref.shape
    band = lax.axis_index("tile")
    count = list_wet(owner_ref, band, want, seen, cols, dests)
    for i in range(7):
        for j in range(7):
            taps[i * 7 + j] = jnp.broadcast_to(taps_in[i, pl.ds(j, 1), :].astype(F32), (8, C))
    cells = convbuf.shape[1]

    def copies(dest, q, b):
        def piece(p, lo, n, lev, nlev, off, width):
            src = stage.at[b, q, pl.ds(lo, n)]
            if nlev > 1:
                src, dst = src.reshape(nlev, width, C), send.at[dest, pl.ds(lev, nlev)]
            else:
                dst = send.at[dest, lev, pl.ds(off, width)]
            return pltpu.make_async_copy(src, dst, sem.at[b, q, p])

        if rows == FULL:
            return [piece(0, 0, 256, 0, 8, 0, 32)]
        if rows == INNER:
            return [piece(0, 0, 16, 1, 1, 16, 16), piece(1, 16, 128, 2, 4, 0, 32),
                    piece(2, 144, 16, 6, 1, 0, 16)]
        return [piece(0, 0, 32, 0, 1, 0, 32), piece(1, 32, 16, 1, 1, 0, 16),
                piece(2, 48, 16, 6, 1, 16, 16), piece(3, 64, 32, 7, 1, 0, 32)]

    def each_copy(k, b, act):
        for q in range(batch):
            index = k * batch + q

            @pl.when(index < count)
            def _():
                for cp in copies(dests[index], q, b):
                    act(cp)

    def convolve(k, q):
        t = cols[k * batch + q]
        own = neighbours(owner_ref, band, t, lon)
        keep = (own[0], None, own[2])
        bias = jnp.broadcast_to(bias_ref[...], (8, C))
        column = pl.ds(pl.multiple_of(t * TS, TS), TS)
        if rows == INNER:
            inbuf[q] = x_ref[pl.ds(3, 10), column, :].reshape(cells, C)
            fill(pad, 0, x_ref, 0, 16, t, lon, keep)
            convbuf[q] = conv_rows(pad, 0, taps, bias, 10).astype(BF16)
            return
        up = neighbours(owner_ref, jnp.maximum(band - 1, 0), t, lon)
        down = neighbours(owner_ref, jnp.minimum(band + 1, bands - 1), t, lon)
        held_rows = x_ref.shape[0]
        fill(pad, 0, top, 0, 3, t, lon, up)
        fill(pad, 3, x_ref, 0, held_rows, t, lon, keep)
        fill(pad, 3 + held_rows, bottom, 0, 3, t, lon, down)
        if rows == FULL:
            inbuf[q] = x_ref[:, column, :].reshape(cells, C)
            convbuf[q] = conv_rows(pad, 0, taps, bias, 16).astype(BF16)
            return
        inbuf[q, pl.ds(0, 48)] = x_ref[pl.ds(0, 3), column, :].reshape(48, C)
        inbuf[q, pl.ds(48, 48)] = x_ref[pl.ds(9, 3), column, :].reshape(48, C)
        convbuf[q, pl.ds(0, 48)] = conv_rows(pad, 0, taps, bias, 3).astype(BF16)
        convbuf[q, pl.ds(48, 48)] = conv_rows(pad, 9, taps, bias, 3).astype(BF16)

    def step(k, _):
        b = lax.rem(k, SLOTS)

        @pl.when(k >= SLOTS)
        def _():
            each_copy(k - SLOTS, b, lambda cp: cp.wait())

        def one(q, _):
            convolve(k, q)
            return 0

        lax.fori_loop(0, jnp.minimum(batch, count - k * batch), one, 0)
        stage[b] = pointwise(
            convbuf[...].reshape(batch * cells, C), inbuf[...].reshape(batch * cells, C),
            gain[...], shift[...], w_in[...], b_in[...], w_out[...], b_out[...], scale[...],
        ).reshape(batch, cells, C)
        each_copy(k, b, lambda cp: cp.start())
        return 0

    batches = lax.div(count + batch - 1, batch)
    lax.fori_loop(0, batches, step, 0)
    for d in range(SLOTS, 0, -1):
        k = batches - d

        @pl.when(k >= 0)
        def _():
            each_copy(k, lax.rem(k, SLOTS), lambda cp: cp.wait())


def block_call(rows, want, batch, owner, x, halos, consts, levels, alias=None, after=None):
    bands, lon = owner.shape
    hbm = pl.BlockSpec(memory_space=pltpu.HBM)
    args = [owner, x, *halos, *consts]
    n_args = len(args)
    held = [pltpu.SMEM(owner.shape, owner.dtype)]
    held.append(pltpu.VMEM((12 if rows == EDGES else x.shape[0],) + x.shape[1:], x.dtype))
    held += [pltpu.VMEM(v.shape, v.dtype) for v in args[2:]]
    passed = [v for v in (alias, after) if v is not None]
    cells = CELLS[rows]
    return pl.pallas_call(
        functools.partial(block_kernel, rows, want, batch, n_args, len(passed)),
        in_specs=[hbm] * (n_args + len(passed)),
        out_specs=hbm,
        out_shape=jax.ShapeDtypeStruct((bands, levels, TS * TS // levels, C), BF16),
        scratch_shapes=held + [
            pltpu.VMEM((22, 32, C), F32),
            pltpu.VMEM((49, 8, C), F32),
            pltpu.VMEM((batch, cells, C), BF16),
            pltpu.VMEM((batch, cells, C), BF16),
            pltpu.VMEM((SLOTS, batch, cells, C), BF16),
            pltpu.SMEM((bands,), jnp.int32),
            pltpu.SMEM((lon + 1,), jnp.int32),
            pltpu.SMEM((lon + 1,), jnp.int32),
            pltpu.SemaphoreType.DMA((SLOTS, batch, 4)),
            pltpu.SemaphoreType.DMA((n_args + 1,)),
        ],
        input_output_aliases={} if alias is None else {n_args: 0},
        compiler_params=pltpu.CompilerParams(vmem_limit_bytes=VMEM_BYTES),
        cost_estimate=pl.CostEstimate(
            flops=bands * cells * C * (2 * 49 + 4 * 512) * 8, transcendentals=bands * cells * 512,
            bytes_accessed=2 * x.size + bands * cells * C * 2),
        name=rows,
    )(*args, *passed)


GROUP = 4


def vertical_kernel(src, rank, recv0, recv1, w_hbm, out, held, done, w, sem_in, sem_out, sem_w):
    tiles, levels, cells = held.shape[:3]

    def each_fetch(t, act):
        for r, recv in enumerate((recv0, recv1)):
            @pl.when(rank[t] == r)
            def _():
                act(pltpu.make_async_copy(recv.at[src[t]], held.at[t], sem_in.at[t]))

    def store(t):
        return pltpu.make_async_copy(done.at[t], out.at[t], sem_out.at[t])

    def start(t, _):
        each_fetch(t, lambda cp: cp.start())
        return 0

    weights = pltpu.make_async_copy(w_hbm, w, sem_w)
    weights.start()
    lax.fori_loop(0, tiles, start, 0)
    weights.wait()

    def step(g, _):
        for q in range(GROUP):
            each_fetch(g * GROUP + q, lambda cp: cp.wait())
        zero = jnp.zeros((2 * cells, C), BF16)
        centre, wide = [], []
        for q in range(GROUP):
            x = held[g * GROUP + q].reshape(levels * cells, C)
            padded = jnp.concatenate([zero, x, zero], axis=0)
            centre.append(x.astype(F32))
            wide.append(jnp.concatenate(
                [padded[k * cells : (k + levels) * cells] for k in range(5)], axis=1))
        total = jnp.concatenate(centre, axis=0) + jnp.dot(
            jnp.concatenate(wide, axis=0), w[...], preferred_element_type=F32)
        done[pl.ds(g * GROUP, GROUP)] = total.astype(BF16).reshape(GROUP, levels, cells, C)
        for q in range(GROUP):
            store(g * GROUP + q).start()
        return 0

    lax.fori_loop(0, tiles // GROUP, step, 0)

    def drain(t, _):
        store(t).wait()
        return 0

    lax.fori_loop(0, tiles, drain, 0)


def vertical_call(src, rank, recv0, recv1, w_vert):
    tiles = src.shape[0]
    levels, cells = recv0.shape[1:3]
    smem = pl.BlockSpec(memory_space=pltpu.SMEM)
    hbm = pl.BlockSpec(memory_space=pltpu.HBM)
    return pl.pallas_call(
        vertical_kernel,
        in_specs=[smem, smem, hbm, hbm, hbm],
        out_specs=hbm,
        out_shape=jax.ShapeDtypeStruct((tiles, levels, cells, C), BF16),
        scratch_shapes=[
            pltpu.VMEM((tiles, levels, cells, C), BF16),
            pltpu.VMEM((tiles, levels, cells, C), BF16),
            pltpu.VMEM((5 * C, C), BF16),
            pltpu.SemaphoreType.DMA((tiles,)),
            pltpu.SemaphoreType.DMA((tiles,)),
            pltpu.SemaphoreType.DMA,
        ],
        compiler_params=pltpu.CompilerParams(vmem_limit_bytes=VMEM_BYTES),
        name="vertical",
    )(src, rank, recv0, recv1, w_vert.reshape(5 * C, C))


def body(ocean_state, tile_owner, kernel, bias_dw, ln_gain, ln_bias, w_in, b_in, w_out, b_out,
         layer_scale, w_vert):
    bands, lon = tile_owner.shape
    levels = lax.axis_size("lev")
    band = lax.axis_index("tile")
    x = ocean_state[0]
    ends = bands - 1
    top = lax.ppermute(x[TS - 3 :], "tile", [(i, i + 1) for i in range(ends)])
    bottom = lax.ppermute(x[:3], "tile", [(i + 1, i) for i in range(ends)])
    row = lambda v: v.reshape(1, -1)
    consts = (kernel, row(bias_dw), row(ln_gain), row(ln_bias), w_in, row(b_in), w_out, row(b_out),
              row(layer_scale))
    halos = (top, bottom)

    def exchange(sent):
        return lax.all_to_all(
            sent.reshape((bands * levels,) + sent.shape[2:]), ("tile", "lev"), split_axis=0,
            concat_axis=0, tiled=True,
        ).reshape(sent.shape)

    sent1 = block_call(INNER, 1, 4, tile_owner, x, (), consts, levels)
    sent1 = block_call(EDGES, 1, 8, tile_owner, x, halos, consts, levels, alias=sent1)
    sent0 = block_call(FULL, 0, 4, tile_owner, x, halos, consts, levels, after=sent1)
    sent0, recv1 = lax.optimization_barrier((sent0, exchange(sent1)))
    recv0 = exchange(sent0)

    owner_of = jnp.where(tile_owner >= 0, tile_owner // bands, -1)
    mine = owner_of == band
    before = jnp.cumsum(mine.astype(jnp.int32), axis=1) - mine
    hit = (tile_owner.reshape(1, -1) == (band * bands + jnp.arange(bands))[:, None])
    code = jnp.arange(bands, dtype=jnp.int32)[:, None] * CAP + before
    found = jnp.sum(jnp.where(hit, code.reshape(1, -1), 0), axis=1)
    return vertical_call(found // CAP, found % CAP, recv0, recv1, w_vert)


def solution(mesh):
    return jax.shard_map(
        body,
        mesh=mesh,
        in_specs=(P("lev", "tile", None, None),) + (P(),) * 11,
        out_specs=P("tile", None, "lev", None),
        check_vma=False,
    )
```

```python
import functools
from fractions import Fraction

import jax
import jax.numpy as jnp
from jax import lax
from jax.experimental import pallas as pl
from jax.experimental.pallas import tpu as pltpu
from jax.sharding import PartitionSpec as P

CAP = 2
TS = 16
C = 128
F32 = jnp.float32
BF16 = jnp.bfloat16
SLOTS = 2
VMEM_BYTES = 63 << 20


def list_wet(owner_ref, band, want, seen, cols, dests):
    bands, lon = owner_ref.shape

    def clear(o, _):
        seen[o] = 0
        return 0

    lax.fori_loop(0, bands, clear, 0)

    def scan(c, count):
        g = owner_ref[band, c]
        dest = lax.shift_right_logical(jnp.maximum(g, 0), bands.bit_length() - 1)
        rank = seen[dest]
        cols[count] = c
        dests[count] = dest
        seen[dest] = rank + (g >= 0).astype(jnp.int32)
        return count + ((g >= 0) & (rank == want)).astype(jnp.int32)

    return lax.fori_loop(0, lon, scan, 0, unroll=4)


def toom_cook():
    pairs = [Fraction(1), Fraction(2), Fraction(1, 2), Fraction(3, 4)]
    squares = [p * p for p in pairs]

    def times(poly, root):
        low = [-root * v for v in poly] + [Fraction(0)]
        high = [Fraction(0)] + list(poly)
        return [p + q for p, q in zip(low, high)]

    def product(roots):
        poly = [Fraction(1)]
        for root in roots:
            poly = times(poly, root)
        return poly

    points = [Fraction(0)] + [v for p in pairs for v in (p, -p)]
    taps = []
    for p in points:
        scale = Fraction(1)
        for q in points:
            if q != p:
                scale = scale * (p - q)
        taps.append([float(p**i / scale) for i in range(7)])
    taps.append([0.0] * 6 + [1.0])
    inner = [[float(v) for v in product([q for q in squares if q != p])] for p in squares]
    whole = [float(v) for v in product(squares)]
    return [float(p) for p in pairs], taps, inner, whole


PAIRS, TAPS, INNER_POLY, WHOLE_POLY = toom_cook()
POINTS = len(TAPS)


def combine(values, coefs):
    total = None
    for v, c in zip(values, coefs):
        term = v if c == 1.0 else v * c
        total = term if total is None else total + term
    return total


def conv_blocks(blocks, wide, taps, bias):
    for m, d in enumerate(blocks):
        values = [combine(d[0:9:2], WHOLE_POLY)]
        for p, poly in zip(PAIRS, INNER_POLY):
            even = combine(d[2:9:2], poly)
            odd = combine(d[1:8:2], poly)
            if p != 1.0:
                odd = odd * p
            values += [even + odd, even - odd]
        values.append(combine(d[1:10:2], WHOLE_POLY))
        for n, v in enumerate(values):
            wide[m, n, pl.ds(0, 8), :] = v[16:]
            wide[m, n, pl.ds(8, 16), :] = v[:16]
            wide[m, n, pl.ds(24, 8), :] = v[16:]
    cells = [(m, h) for m in range(len(blocks)) for h in range(2)]

    def product(n):
        total = [None] * len(cells)
        for j in range(7):
            tap = taps[n * 7 + j]
            for i, (m, h) in enumerate(cells):
                term = wide[m, n, pl.ds(5 + j + 8 * h, 8), :] * tap
                total[i] = term if j == 0 else total[i] + term
        return total

    y = [[v + bias for v in product(0)]] + [[bias] * len(cells) for _ in range(3)]
    for q, p in enumerate(PAIRS):
        plus, minus = product(1 + 2 * q), product(2 + 2 * q)
        for i in range(len(cells)):
            s, t = plus[i] + minus[i], plus[i] - minus[i]
            y[0][i] = y[0][i] + s
            y[1][i] = y[1][i] + (t if p == 1.0 else t * p)
            y[2][i] = y[2][i] + (s if p == 1.0 else s * (p * p))
            y[3][i] = y[3][i] + (t if p == 1.0 else t * (p * p * p))
    last = product(POINTS - 1)
    y[3] = [v + w for v, w in zip(y[3], last)]
    return [[jnp.concatenate([y[r][2 * m], y[r][2 * m + 1]], axis=0) for r in range(4)]
            for m in range(len(blocks))]


def pointwise(conv, inp, gain, shift, w_in, b_in, w_out, b_out, scale):
    values = conv.astype(F32)
    centre = jnp.mean(values, axis=-1, keepdims=True)
    dev = values - centre
    spread = jnp.mean(dev * dev, axis=-1, keepdims=True)
    normed = (dev * lax.rsqrt(spread + 1e-06) * gain + shift).astype(BF16)
    h = jnp.dot(normed, w_in, preferred_element_type=F32) + b_in
    half = 0.5 * h
    hidden = (half + half * lax.erf(h * 0.7071067811865476)).astype(BF16)
    branch = jnp.dot(hidden, w_out, preferred_element_type=F32) + b_out
    return (inp.astype(F32) + scale * branch).astype(BF16)


def window_rows(src, rows, t, lon, keep):
    left = lax.rem(t + lon - 1, lon)
    right = lax.rem(t + 1, lon)
    keep_l, keep_c, keep_r = keep
    zero = jnp.zeros((), F32)
    first = lax.broadcasted_iota(jnp.int32, (8, C), 0) < 4
    keep_side = jnp.where(first, keep_r.astype(F32), keep_l.astype(F32)) > 0

    def tile(r, col):
        return src[r, pl.ds(pl.multiple_of(col * TS, TS), TS), :].astype(F32)

    out = []
    for r in rows:
        centre = tile(r, t)
        if keep_c is not None:
            centre = jnp.where(keep_c, centre, zero)
        side = jnp.where(first, tile(r, right)[:8], tile(r, left)[8:])
        out.append(jnp.concatenate([centre, jnp.where(keep_side, side, zero)], axis=0))
    return out


def neighbours(owner_ref, band, t, lon):
    left = lax.rem(t + lon - 1, lon)
    right = lax.rem(t + 1, lon)
    return (owner_ref[band, left] >= 0, owner_ref[band, t] >= 0, owner_ref[band, right] >= 0)


INNER, EDGES, FULL = "inner_rows", "edge_rows", "full_rows"
CELLS = {INNER: 128, EDGES: 128, FULL: 256}


def block_kernel(rows, want, batch, n_args, n_pass, *refs):
    args, refs = refs[:n_args], refs[n_args + n_pass :]
    send, refs = refs[0], refs[1:]
    held, refs = refs[:n_args], refs[n_args:]
    wide, taps, convbuf, inbuf, stage, seen, cols, dests, sem, load = refs
    loads = []
    for q, (src, dst) in enumerate(zip(args, held)):
        if rows == EDGES and q == 1:
            loads.append(pltpu.make_async_copy(src.at[pl.ds(0, 7)], dst.at[pl.ds(0, 7)], load.at[q]))
            loads.append(pltpu.make_async_copy(src.at[pl.ds(9, 7)], dst.at[pl.ds(7, 7)], load.at[n_args]))
        else:
            loads.append(pltpu.make_async_copy(src, dst, load.at[q]))
    for cp in loads:
        cp.start()
    owner_ref, x_ref = held[:2]
    if rows != INNER:
        top, bottom = held[2:4]
    taps_in, bias_ref, gain, shift, w_in, b_in, w_out, b_out, scale = held[-9:]
    bands, lon = owner_ref.shape
    band = lax.axis_index("tile")
    loads[0].wait()
    count = list_wet(owner_ref, band, want, seen, cols, dests)
    loads[-9].wait()
    for j in range(7):
        column_taps = [
            jnp.broadcast_to(taps_in[i, pl.ds(j, 1), :].astype(F32), (8, C)) for i in range(7)]
        for n in range(POINTS):
            used = [(k, c) for k, c in zip(column_taps, TAPS[n]) if c != 0.0]
            total = combine(*zip(*used))
            taps[n * 7 + j] = total
    for cp in loads[1:-9] + loads[-8:]:
        cp.wait()
    cells = convbuf.shape[1]

    def copies(dest, q, b):
        def piece(p, lo, n, lev):
            return pltpu.make_async_copy(
                stage.at[b, q, pl.ds(lo, n)], send.at[dest, pl.ds(lev, n)], sem.at[b, q, p])

        half = send.shape[1] // 2
        if rows == FULL:
            return [piece(0, 0, 2 * half, 0)]
        if rows == INNER:
            return [piece(0, 0, half, half // 2)]
        return [piece(0, 0, half // 2, 0), piece(1, half // 2, half // 2, half + half // 2)]

    def each_copy(k, b, act):
        for q in range(batch):
            index = k * batch + q

            @pl.when(index < count)
            def _():
                for cp in copies(dests[index], q, b):
                    act(cp)

    def convolve(k, q):
        t = cols[k * batch + q]
        own = neighbours(owner_ref, band, t, lon)
        own = (own[0], None, own[2])
        bias = jnp.broadcast_to(bias_ref[...], (8, C))
        column = pl.ds(pl.multiple_of(t * TS, TS), TS)

        def window(src, picked, keep=own):
            return window_rows(src, picked, t, lon, keep)

        def above(n):
            up = neighbours(owner_ref, jnp.maximum(band - 1, 0), t, lon)
            return window(top, range(3), up) + window(x_ref, range(n))

        def below(n):
            down = neighbours(owner_ref, jnp.minimum(band + 1, bands - 1), t, lon)
            last = x_ref.shape[0]
            return window(x_ref, range(last - n, last)) + window(bottom, range(3), down)

        def put(first, blocks):
            for n, block in enumerate(conv_blocks(blocks, wide, taps, bias)):
                for r, out in enumerate(block):
                    convbuf[q, pl.ds((first + n * 4 + r) * TS, TS)] = out.astype(BF16)

        if rows == INNER:
            cut = window(x_ref, range(1, 15))
            put(0, [cut[:10], cut[4:]])
            inbuf[q] = x_ref[pl.ds(4, 8), column, :].reshape(cells, C)
        elif rows == EDGES:
            put(0, [above(7), below(7)])
            inbuf[q, pl.ds(0, 64)] = x_ref[pl.ds(0, 4), column, :].reshape(64, C)
            inbuf[q, pl.ds(64, 64)] = x_ref[pl.ds(10, 4), column, :].reshape(64, C)
        else:
            cut = above(11)
            put(0, [cut[:10], cut[4:]])
            cut = below(11)
            put(8, [cut[:10], cut[4:]])
            inbuf[q] = x_ref[:, column, :].reshape(cells, C)

    def step(k, _):
        b = lax.rem(k, SLOTS)

        @pl.when(k >= SLOTS)
        def _():
            each_copy(k - SLOTS, b, lambda cp: cp.wait())

        def one(q, _):
            convolve(k, q)
            return 0

        lax.fori_loop(0, jnp.minimum(batch, count - k * batch), one, 0)
        tiles = 512 // cells
        for part in range(0, batch, tiles):
            piece = pl.ds(part, tiles)
            stage[b, piece] = pointwise(
                convbuf[piece].reshape(512, C), inbuf[piece].reshape(512, C), gain[...], shift[...],
                w_in[...], b_in[...], w_out[...], b_out[...], scale[...],
            ).reshape((tiles,) + stage.shape[2:])
        each_copy(k, b, lambda cp: cp.start())
        return 0

    batches = lax.div(count + batch - 1, batch)
    lax.fori_loop(0, batches, step, 0)
    for d in range(SLOTS, 0, -1):
        k = batches - d

        @pl.when(k >= 0)
        def _():
            each_copy(k, lax.rem(k, SLOTS), lambda cp: cp.wait())


def block_call(rows, want, batch, owner, x, halos, consts, levels, alias=None, after=None):
    bands, lon = owner.shape
    hbm = pl.BlockSpec(memory_space=pltpu.HBM)
    args = [owner, x, *halos, *consts]
    n_args = len(args)
    held = [pltpu.SMEM(owner.shape, owner.dtype)]
    held.append(pltpu.VMEM((14 if rows == EDGES else x.shape[0],) + x.shape[1:], x.dtype))
    held += [pltpu.VMEM(v.shape, v.dtype) for v in args[2:]]
    passed = [v for v in (alias, after) if v is not None]
    cells = CELLS[rows]
    share = TS * TS // levels
    return pl.pallas_call(
        functools.partial(block_kernel, rows, want, batch, n_args, len(passed)),
        in_specs=[hbm] * (n_args + len(passed)),
        out_specs=hbm,
        out_shape=jax.ShapeDtypeStruct((bands, levels, share, C), BF16),
        scratch_shapes=held + [
            pltpu.VMEM((2, POINTS, 32, C), F32),
            pltpu.VMEM((POINTS * 7, 8, C), F32),
            pltpu.VMEM((batch, cells, C), BF16),
            pltpu.VMEM((batch, cells, C), BF16),
            pltpu.VMEM((SLOTS, batch, cells // share, share, C), BF16),
            pltpu.SMEM((bands,), jnp.int32),
            pltpu.SMEM((lon + 1,), jnp.int32),
            pltpu.SMEM((lon + 1,), jnp.int32),
            pltpu.SemaphoreType.DMA((SLOTS, batch, 2)),
            pltpu.SemaphoreType.DMA((n_args + 1,)),
        ],
        input_output_aliases={} if alias is None else {n_args: 0},
        compiler_params=pltpu.CompilerParams(vmem_limit_bytes=VMEM_BYTES),
        cost_estimate=pl.CostEstimate(
            flops=bands * cells * C * (2 * 49 + 4 * 512) * 8, transcendentals=bands * cells * 512,
            bytes_accessed=2 * x.size + bands * cells * C * 2),
        name=rows,
    )(*args, *passed)


GROUP = 4


def vertical_kernel(src, rank, recv0, recv1, w_hbm, out, held, done, taps, w, sem_in,
                    sem_out, sem_w):
    tiles, levels, cells = held.shape[:3]

    def each_fetch(t, act):
        for r, recv in enumerate((recv0, recv1)):
            @pl.when(rank[t] == r)
            def _():
                act(pltpu.make_async_copy(recv.at[src[t]], held.at[t], sem_in.at[t]))

    def store(t):
        return pltpu.make_async_copy(done.at[t], out.at[t], sem_out.at[t])

    def start(t, _):
        each_fetch(t, lambda cp: cp.start())
        return 0

    weights = pltpu.make_async_copy(w_hbm, taps, sem_w)
    weights.start()
    lax.fori_loop(0, tiles, start, 0)
    weights.wait()
    for d in range(6):
        for p in range(2):
            k = d - p
            block = taps[k] if 0 <= k < 5 else jnp.zeros((C, C), BF16)
            w[pl.ds(d * C, C), pl.ds(p * C, C)] = block

    def step(g, _):
        for q in range(GROUP):
            each_fetch(g * GROUP + q, lambda cp: cp.wait())
        zero = jnp.zeros((cells, C), BF16)
        wide = []
        for q in range(GROUP):
            x = [zero, zero] + [held[g * GROUP + q, lev] for lev in range(levels)] + [zero, zero]
            wide += [jnp.concatenate(x[lev : lev + 6], axis=1) for lev in range(0, levels, 2)]
        total = jnp.dot(jnp.concatenate(wide, axis=0), w[...], preferred_element_type=F32)
        for q in range(GROUP):
            t = g * GROUP + q
            for lev in range(levels):
                row = (q * levels // 2 + lev // 2) * cells
                part = total[row : row + cells, (lev % 2) * C : (lev % 2 + 1) * C]
                done[t, lev] = (held[t, lev].astype(F32) + part).astype(BF16)
            store(t).start()
        return 0

    lax.fori_loop(0, tiles // GROUP, step, 0)

    def drain(t, _):
        store(t).wait()
        return 0

    lax.fori_loop(0, tiles, drain, 0)


def vertical_call(src, rank, recv0, recv1, w_vert):
    tiles = src.shape[0]
    levels, cells = recv0.shape[1:3]
    smem = pl.BlockSpec(memory_space=pltpu.SMEM)
    hbm = pl.BlockSpec(memory_space=pltpu.HBM)
    return pl.pallas_call(
        vertical_kernel,
        in_specs=[smem, smem, hbm, hbm, hbm],
        out_specs=hbm,
        out_shape=jax.ShapeDtypeStruct((tiles, levels, cells, C), BF16),
        scratch_shapes=[
            pltpu.VMEM((tiles, levels, cells, C), BF16),
            pltpu.VMEM((tiles, levels, cells, C), BF16),
            pltpu.VMEM((5, C, C), BF16),
            pltpu.VMEM((6 * C, 2 * C), BF16),
            pltpu.SemaphoreType.DMA((tiles,)),
            pltpu.SemaphoreType.DMA((tiles,)),
            pltpu.SemaphoreType.DMA,
        ],
        compiler_params=pltpu.CompilerParams(vmem_limit_bytes=VMEM_BYTES),
        name="vertical",
    )(src, rank, recv0, recv1, w_vert)


def body(ocean_state, tile_owner, kernel, bias_dw, ln_gain, ln_bias, w_in, b_in, w_out, b_out,
         layer_scale, w_vert):
    bands, lon = tile_owner.shape
    levels = lax.axis_size("lev")
    band = lax.axis_index("tile")
    x = ocean_state[0]
    ends = bands - 1
    top = lax.ppermute(x[TS - 3 :], "tile", [(i, i + 1) for i in range(ends)])
    bottom = lax.ppermute(x[:3], "tile", [(i + 1, i) for i in range(ends)])
    row = lambda v: v.reshape(1, -1)
    consts = (kernel, row(bias_dw), row(ln_gain), row(ln_bias), w_in, row(b_in), w_out, row(b_out),
              row(layer_scale))
    halos = (top, bottom)

    def exchange(sent):
        return lax.all_to_all(
            sent.reshape((bands * levels,) + sent.shape[2:]), ("tile", "lev"), split_axis=0,
            concat_axis=0, tiled=True,
        ).reshape(sent.shape)

    sent1 = block_call(INNER, 1, 4, tile_owner, x, (), consts, levels)
    sent1 = block_call(EDGES, 1, 4, tile_owner, x, halos, consts, levels, alias=sent1)
    sent0 = block_call(FULL, 0, 4, tile_owner, x, halos, consts, levels, after=sent1)
    sent0, recv1 = lax.optimization_barrier((sent0, exchange(sent1)))
    recv0 = exchange(sent0)

    owner_of = jnp.where(tile_owner >= 0, tile_owner // bands, -1)
    mine = owner_of == band
    before = jnp.cumsum(mine.astype(jnp.int32), axis=1) - mine
    hit = (tile_owner.reshape(1, -1) == (band * bands + jnp.arange(bands))[:, None])
    code = jnp.arange(bands, dtype=jnp.int32)[:, None] * CAP + before
    found = jnp.sum(jnp.where(hit, code.reshape(1, -1), 0), axis=1)
    return vertical_call(found // CAP, found % CAP, recv0, recv1, w_vert)


def solution(mesh):
    return jax.shard_map(
        body,
        mesh=mesh,
        in_specs=(P("lev", "tile", None, None),) + (P(),) * 11,
        out_specs=P("tile", None, "lev", None),
        check_vma=False,
    )
```

```python
import functools
from fractions import Fraction

import jax
import jax.numpy as jnp
from jax import lax
from jax.experimental import pallas as pl
from jax.experimental.pallas import tpu as pltpu
from jax.sharding import PartitionSpec as P

CAP = 2
TS = 16
C = 128
F32 = jnp.float32
BF16 = jnp.bfloat16
SLOTS = 2
VMEM_BYTES = 63 << 20


def list_wet(owner_ref, band, want, seen, cols, dests):
    bands, lon = owner_ref.shape

    def clear(o, _):
        seen[o] = 0
        return 0

    lax.fori_loop(0, bands, clear, 0)

    def scan(c, count):
        g = owner_ref[band, c]
        dest = lax.shift_right_logical(jnp.maximum(g, 0), bands.bit_length() - 1)
        rank = seen[dest]
        cols[count] = c
        dests[count] = dest
        seen[dest] = rank + (g >= 0).astype(jnp.int32)
        return count + ((g >= 0) & (rank == want)).astype(jnp.int32)

    return lax.fori_loop(0, lon, scan, 0, unroll=4)


def toom_cook():
    pairs = [Fraction(1), Fraction(2), Fraction(1, 2), Fraction(3, 4)]
    squares = [p * p for p in pairs]

    def times(poly, root):
        low = [-root * v for v in poly] + [Fraction(0)]
        high = [Fraction(0)] + list(poly)
        return [p + q for p, q in zip(low, high)]

    def product(roots):
        poly = [Fraction(1)]
        for root in roots:
            poly = times(poly, root)
        return poly

    points = [Fraction(0)] + [v for p in pairs for v in (p, -p)]
    taps = []
    for p in points:
        scale = Fraction(1)
        for q in points:
            if q != p:
                scale = scale * (p - q)
        taps.append([float(p**i / scale) for i in range(7)])
    taps.append([0.0] * 6 + [1.0])
    inner = [[float(v) for v in product([q for q in squares if q != p])] for p in squares]
    whole = [float(v) for v in product(squares)]
    return [float(p) for p in pairs], taps, inner, whole


PAIRS, TAPS, INNER_POLY, WHOLE_POLY = toom_cook()
POINTS = len(TAPS)


def combine(values, coefs):
    total = None
    for v, c in zip(values, coefs):
        term = v if c == 1.0 else v * c
        total = term if total is None else total + term
    return total


def conv_blocks(blocks, wide, taps, bias):
    for m, d in enumerate(blocks):
        values = [combine(d[0:9:2], WHOLE_POLY)]
        for p, poly in zip(PAIRS, INNER_POLY):
            even = combine(d[2:9:2], poly)
            odd = combine(d[1:8:2], poly)
            if p != 1.0:
                odd = odd * p
            values += [even + odd, even - odd]
        values.append(combine(d[1:10:2], WHOLE_POLY))
        for n, v in enumerate(values):
            wide[m, n, pl.ds(0, 8), :] = v[16:]
            wide[m, n, pl.ds(8, 16), :] = v[:16]
            wide[m, n, pl.ds(24, 8), :] = v[16:]
    cells = [(m, h) for m in range(len(blocks)) for h in range(2)]

    def product(n):
        total = [None] * len(cells)
        for j in range(7):
            tap = taps[n * 7 + j]
            for i, (m, h) in enumerate(cells):
                term = wide[m, n, pl.ds(5 + j + 8 * h, 8), :] * tap
                total[i] = term if j == 0 else total[i] + term
        return total

    y = [[v + bias for v in product(0)]] + [[bias] * len(cells) for _ in range(3)]
    for q, p in enumerate(PAIRS):
        plus, minus = product(1 + 2 * q), product(2 + 2 * q)
        for i in range(len(cells)):
            s, t = plus[i] + minus[i], plus[i] - minus[i]
            y[0][i] = y[0][i] + s
            y[1][i] = y[1][i] + (t if p == 1.0 else t * p)
            y[2][i] = y[2][i] + (s if p == 1.0 else s * (p * p))
            y[3][i] = y[3][i] + (t if p == 1.0 else t * (p * p * p))
    last = product(POINTS - 1)
    y[3] = [v + w for v, w in zip(y[3], last)]
    return [[jnp.concatenate([y[r][2 * m], y[r][2 * m + 1]], axis=0) for r in range(4)]
            for m in range(len(blocks))]


def pointwise(conv, inp, gain, shift, w_in, b_in, w_out, b_out, scale):
    values = conv.astype(F32)
    centre = jnp.mean(values, axis=-1, keepdims=True)
    dev = values - centre
    spread = jnp.mean(dev * dev, axis=-1, keepdims=True)
    normed = (dev * lax.rsqrt(spread + 1e-06) * gain + shift).astype(BF16)
    h = jnp.dot(normed, w_in, preferred_element_type=F32) + b_in
    half = 0.5 * h
    hidden = (half + half * lax.erf(h * 0.7071067811865476)).astype(BF16)
    branch = jnp.dot(hidden, w_out, preferred_element_type=F32) + b_out
    return (inp.astype(F32) + scale * branch).astype(BF16)


def window_rows(src, rows, t, lon, keep):
    left = lax.rem(t + lon - 1, lon)
    right = lax.rem(t + 1, lon)
    keep_l, keep_c, keep_r = keep
    zero = jnp.zeros((), F32)
    first = lax.broadcasted_iota(jnp.int32, (8, C), 0) < 4
    keep_side = jnp.where(first, keep_r.astype(F32), keep_l.astype(F32)) > 0

    def tile(r, col):
        return src[r, pl.ds(pl.multiple_of(col * TS, TS), TS), :].astype(F32)

    out = []
    for r in rows:
        centre = tile(r, t)
        if keep_c is not None:
            centre = jnp.where(keep_c, centre, zero)
        side = jnp.where(first, tile(r, right)[:8], tile(r, left)[8:])
        out.append(jnp.concatenate([centre, jnp.where(keep_side, side, zero)], axis=0))
    return out


def neighbours(owner_ref, band, t, lon):
    left = lax.rem(t + lon - 1, lon)
    right = lax.rem(t + 1, lon)
    return (owner_ref[band, left] >= 0, owner_ref[band, t] >= 0, owner_ref[band, right] >= 0)


INNER, EDGES, FULL = "inner_rows", "edge_rows", "full_rows"
CELLS = {INNER: 128, EDGES: 128, FULL: 256}


def block_kernel(rows, want, batch, n_args, n_pass, *refs):
    args, refs = refs[:n_args], refs[n_args + n_pass :]
    send, refs = refs[0], refs[1:]
    held, refs = refs[:n_args], refs[n_args:]
    wide, taps, convbuf, inbuf, stage, seen, cols, dests, sem, load = refs
    loads = []
    for q, (src, dst) in enumerate(zip(args, held)):
        if rows == EDGES and q == 1:
            loads.append(pltpu.make_async_copy(src.at[pl.ds(0, 7)], dst.at[pl.ds(0, 7)], load.at[q]))
            loads.append(pltpu.make_async_copy(src.at[pl.ds(9, 7)], dst.at[pl.ds(7, 7)], load.at[n_args]))
        else:
            loads.append(pltpu.make_async_copy(src, dst, load.at[q]))
    for cp in loads:
        cp.start()
    owner_ref, x_ref = held[:2]
    if rows != INNER:
        top, bottom = held[2:4]
    taps_in, bias_ref, gain, shift, w_in, b_in, w_out, b_out, scale = held[-9:]
    bands, lon = owner_ref.shape
    band = lax.axis_index("tile")
    loads[0].wait()
    count = list_wet(owner_ref, band, want, seen, cols, dests)
    loads[-9].wait()
    for j in range(7):
        column_taps = [
            jnp.broadcast_to(taps_in[i, pl.ds(j, 1), :].astype(F32), (8, C)) for i in range(7)]
        for n in range(POINTS):
            used = [(k, c) for k, c in zip(column_taps, TAPS[n]) if c != 0.0]
            total = combine(*zip(*used))
            taps[n * 7 + j] = total
    for cp in loads[1:-9] + loads[-8:]:
        cp.wait()
    cells = convbuf.shape[1]

    def copies(dest, q, b):
        def piece(p, lo, n, lev):
            return pltpu.make_async_copy(
                stage.at[b, q, pl.ds(lo, n)], send.at[dest, pl.ds(lev, n)], sem.at[b, q, p])

        half = send.shape[1] // 2
        if rows == FULL:
            return [piece(0, 0, 2 * half, 0)]
        if rows == INNER:
            return [piece(0, 0, half, half // 2)]
        return [piece(0, 0, half // 2, 0), piece(1, half // 2, half // 2, half + half // 2)]

    def each_copy(k, b, act):
        for q in range(batch):
            index = k * batch + q

            @pl.when(index < count)
            def _():
                for cp in copies(dests[index], q, b):
                    act(cp)

    def convolve(k, q):
        t = cols[k * batch + q]
        own = neighbours(owner_ref, band, t, lon)
        own = (own[0], None, own[2])
        bias = jnp.broadcast_to(bias_ref[...], (8, C))
        column = pl.ds(pl.multiple_of(t * TS, TS), TS)

        def window(src, picked, keep=own):
            return window_rows(src, picked, t, lon, keep)

        def above(n):
            up = neighbours(owner_ref, jnp.maximum(band - 1, 0), t, lon)
            return window(top, range(3), up) + window(x_ref, range(n))

        def below(n):
            down = neighbours(owner_ref, jnp.minimum(band + 1, bands - 1), t, lon)
            last = x_ref.shape[0]
            return window(x_ref, range(last - n, last)) + window(bottom, range(3), down)

        def put(first, blocks):
            for n, block in enumerate(conv_blocks(blocks, wide, taps, bias)):
                for r, out in enumerate(block):
                    convbuf[q, pl.ds((first + n * 4 + r) * TS, TS)] = out.astype(BF16)

        if rows == INNER:
            cut = window(x_ref, range(1, 15))
            put(0, [cut[:10], cut[4:]])
            inbuf[q] = x_ref[pl.ds(4, 8), column, :].reshape(cells, C)
        elif rows == EDGES:
            put(0, [above(7), below(7)])
            inbuf[q, pl.ds(0, 64)] = x_ref[pl.ds(0, 4), column, :].reshape(64, C)
            inbuf[q, pl.ds(64, 64)] = x_ref[pl.ds(10, 4), column, :].reshape(64, C)
        else:
            cut = above(11)
            put(0, [cut[:10], cut[4:]])
            cut = below(11)
            put(8, [cut[:10], cut[4:]])
            inbuf[q] = x_ref[:, column, :].reshape(cells, C)

    def step(k, _):
        b = lax.rem(k, SLOTS)

        @pl.when(k >= SLOTS)
        def _():
            each_copy(k - SLOTS, b, lambda cp: cp.wait())

        def one(q, _):
            convolve(k, q)
            return 0

        lax.fori_loop(0, jnp.minimum(batch, count - k * batch), one, 0)
        tiles = 512 // cells
        for part in range(0, batch, tiles):
            piece = pl.ds(part, tiles)
            stage[b, piece] = pointwise(
                convbuf[piece].reshape(512, C), inbuf[piece].reshape(512, C), gain[...], shift[...],
                w_in[...], b_in[...], w_out[...], b_out[...], scale[...],
            ).reshape((tiles,) + stage.shape[2:])
        each_copy(k, b, lambda cp: cp.start())
        return 0

    batches = lax.div(count + batch - 1, batch)
    lax.fori_loop(0, batches, step, 0)
    for d in range(SLOTS, 0, -1):
        k = batches - d

        @pl.when(k >= 0)
        def _():
            each_copy(k, lax.rem(k, SLOTS), lambda cp: cp.wait())


def block_call(rows, want, batch, owner, x, halos, consts, levels, alias=None, after=None):
    bands, lon = owner.shape
    hbm = pl.BlockSpec(memory_space=pltpu.HBM)
    args = [owner, x, *halos, *consts]
    n_args = len(args)
    held = [pltpu.SMEM(owner.shape, owner.dtype)]
    held.append(pltpu.VMEM((14 if rows == EDGES else x.shape[0],) + x.shape[1:], x.dtype))
    held += [pltpu.VMEM(v.shape, v.dtype) for v in args[2:]]
    passed = [v for v in (alias, after) if v is not None]
    cells = CELLS[rows]
    share = TS * TS // levels
    return pl.pallas_call(
        functools.partial(block_kernel, rows, want, batch, n_args, len(passed)),
        in_specs=[hbm] * (n_args + len(passed)),
        out_specs=hbm,
        out_shape=jax.ShapeDtypeStruct((bands, levels, share, C), BF16),
        scratch_shapes=held + [
            pltpu.VMEM((2, POINTS, 32, C), F32),
            pltpu.VMEM((POINTS * 7, 8, C), F32),
            pltpu.VMEM((batch, cells, C), BF16),
            pltpu.VMEM((batch, cells, C), BF16),
            pltpu.VMEM((SLOTS, batch, cells // share, share, C), BF16),
            pltpu.SMEM((bands,), jnp.int32),
            pltpu.SMEM((lon + 1,), jnp.int32),
            pltpu.SMEM((lon + 1,), jnp.int32),
            pltpu.SemaphoreType.DMA((SLOTS, batch, 2)),
            pltpu.SemaphoreType.DMA((n_args + 1,)),
        ],
        input_output_aliases={} if alias is None else {n_args: 0},
        compiler_params=pltpu.CompilerParams(vmem_limit_bytes=VMEM_BYTES),
        cost_estimate=pl.CostEstimate(
            flops=bands * cells * C * (2 * 49 + 4 * 512) * 8, transcendentals=bands * cells * 512,
            bytes_accessed=2 * x.size + bands * cells * C * 2),
        name=rows,
    )(*args, *passed)


GROUP = 8


def vertical_kernel(src, rank, recv0, recv1, w_hbm, out, held, done, taps, w, sem_in,
                    sem_out, sem_w):
    tiles, levels, cells = held.shape[:3]

    def each_fetch(t, act):
        for r, recv in enumerate((recv0, recv1)):
            @pl.when(rank[t] == r)
            def _():
                act(pltpu.make_async_copy(recv.at[src[t]], held.at[t], sem_in.at[t]))

    def store(t):
        return pltpu.make_async_copy(done.at[t], out.at[t], sem_out.at[t])

    def start(t, _):
        each_fetch(t, lambda cp: cp.start())
        return 0

    weights = pltpu.make_async_copy(w_hbm, taps, sem_w)
    weights.start()
    lax.fori_loop(0, tiles, start, 0, unroll=8)
    weights.wait()
    for d in range(6):
        for p in range(2):
            k = d - p
            block = taps[k] if 0 <= k < 5 else jnp.zeros((C, C), BF16)
            w[pl.ds(d * C, C), pl.ds(p * C, C)] = block

    def step(g, _):
        for q in range(GROUP):
            each_fetch(g * GROUP + q, lambda cp: cp.wait())
        zero = jnp.zeros((cells, C), BF16)
        wide = []
        for q in range(GROUP):
            x = [zero, zero] + [held[g * GROUP + q, lev] for lev in range(levels)] + [zero, zero]
            wide += [jnp.concatenate(x[lev : lev + 6], axis=1) for lev in range(0, levels, 2)]
        total = jnp.dot(jnp.concatenate(wide, axis=0), w[...], preferred_element_type=F32)
        for q in range(GROUP):
            t = g * GROUP + q
            for lev in range(levels):
                row = (q * levels // 2 + lev // 2) * cells
                part = total[row : row + cells, (lev % 2) * C : (lev % 2 + 1) * C]
                done[t, lev] = (held[t, lev].astype(F32) + part).astype(BF16)
            store(t).start()
        return 0

    lax.fori_loop(0, tiles // GROUP, step, 0)

    def drain(t, _):
        store(t).wait()
        return 0

    lax.fori_loop(0, tiles, drain, 0)


def vertical_call(src, rank, recv0, recv1, w_vert):
    tiles = src.shape[0]
    levels, cells = recv0.shape[1:3]
    smem = pl.BlockSpec(memory_space=pltpu.SMEM)
    hbm = pl.BlockSpec(memory_space=pltpu.HBM)
    return pl.pallas_call(
        vertical_kernel,
        in_specs=[smem, smem, hbm, hbm, hbm],
        out_specs=hbm,
        out_shape=jax.ShapeDtypeStruct((tiles, levels, cells, C), BF16),
        scratch_shapes=[
            pltpu.VMEM((tiles, levels, cells, C), BF16),
            pltpu.VMEM((tiles, levels, cells, C), BF16),
            pltpu.VMEM((5, C, C), BF16),
            pltpu.VMEM((6 * C, 2 * C), BF16),
            pltpu.SemaphoreType.DMA((tiles,)),
            pltpu.SemaphoreType.DMA((tiles,)),
            pltpu.SemaphoreType.DMA,
        ],
        compiler_params=pltpu.CompilerParams(vmem_limit_bytes=VMEM_BYTES),
        name="vertical",
    )(src, rank, recv0, recv1, w_vert)


def halo_kernel(x, first, last, held, sem):
    rows = first.shape[0]
    ends = [(0, first), (x.shape[0] - rows, last)]
    loads = [pltpu.make_async_copy(x.at[pl.ds(row, rows)], held.at[q], sem.at[q])
             for q, (row, _) in enumerate(ends)]
    stores = [pltpu.make_async_copy(held.at[q], out, sem.at[2 + q])
              for q, (_, out) in enumerate(ends)]
    for cp in loads:
        cp.start()
    for load, store in zip(loads, stores):
        load.wait()
        store.start()
    for cp in stores:
        cp.wait()


def halo_call(x, rows):
    hbm = pl.BlockSpec(memory_space=pltpu.HBM)
    shape = jax.ShapeDtypeStruct((rows,) + x.shape[1:], x.dtype)
    return pl.pallas_call(
        halo_kernel,
        in_specs=[hbm],
        out_specs=[hbm] * 2,
        out_shape=[shape] * 2,
        scratch_shapes=[pltpu.VMEM((2, rows) + x.shape[1:], x.dtype), pltpu.SemaphoreType.DMA((4,))],
        compiler_params=pltpu.CompilerParams(vmem_limit_bytes=VMEM_BYTES),
        name="halo_rows",
    )(x)


def body(ocean_state, tile_owner, kernel, bias_dw, ln_gain, ln_bias, w_in, b_in, w_out, b_out,
         layer_scale, w_vert):
    bands, lon = tile_owner.shape
    levels = lax.axis_size("lev")
    band = lax.axis_index("tile")
    x = ocean_state[0]
    ends = bands - 1
    head, tail = halo_call(x, 3)
    top = lax.ppermute(tail, "tile", [(i, i + 1) for i in range(ends)])
    bottom = lax.ppermute(head, "tile", [(i + 1, i) for i in range(ends)])
    row = lambda v: v.reshape(1, -1)
    consts = (kernel, row(bias_dw), row(ln_gain), row(ln_bias), w_in, row(b_in), w_out, row(b_out),
              row(layer_scale))
    halos = (top, bottom)

    def exchange(sent):
        return lax.all_to_all(
            sent.reshape((bands * levels,) + sent.shape[2:]), ("tile", "lev"), split_axis=0,
            concat_axis=0, tiled=True,
        ).reshape(sent.shape)

    sent1 = block_call(INNER, 1, 4, tile_owner, x, (), consts, levels)
    sent1 = block_call(EDGES, 1, 4, tile_owner, x, halos, consts, levels, alias=sent1)
    sent0 = block_call(FULL, 0, 4, tile_owner, x, halos, consts, levels, after=sent1)
    sent0, recv1 = lax.optimization_barrier((sent0, exchange(sent1)))
    recv0 = exchange(sent0)

    owner_of = jnp.where(tile_owner >= 0, tile_owner // bands, -1)
    mine = owner_of == band
    before = jnp.cumsum(mine.astype(jnp.int32), axis=1) - mine
    hit = (tile_owner.reshape(1, -1) == (band * bands + jnp.arange(bands))[:, None])
    code = jnp.arange(bands, dtype=jnp.int32)[:, None] * CAP + before
    found = jnp.sum(jnp.where(hit, code.reshape(1, -1), 0), axis=1)
    return vertical_call(found // CAP, found % CAP, recv0, recv1, w_vert)


def solution(mesh):
    return jax.shard_map(
        body,
        mesh=mesh,
        in_specs=(P("lev", "tile", None, None),) + (P(),) * 11,
        out_specs=P("tile", None, "lev", None),
        check_vma=False,
    )
```

```python
import functools
from fractions import Fraction

import jax
import jax.numpy as jnp
from jax import lax
from jax.experimental import pallas as pl
from jax.experimental.pallas import tpu as pltpu
from jax.sharding import PartitionSpec as P

CAP = 2
TS = 16
C = 128
F32 = jnp.float32
BF16 = jnp.bfloat16
SLOTS = 2
VMEM_BYTES = 63 << 20


def list_wet(owner_ref, band, want, seen, cols, dests):
    bands, lon = owner_ref.shape

    def clear(o, _):
        seen[o] = 0
        return 0

    lax.fori_loop(0, bands, clear, 0)

    def scan(c, count):
        g = owner_ref[band, c]
        dest = lax.shift_right_logical(jnp.maximum(g, 0), bands.bit_length() - 1)
        rank = seen[dest]
        cols[count] = c
        dests[count] = dest
        seen[dest] = rank + (g >= 0).astype(jnp.int32)
        return count + ((g >= 0) & (rank == want)).astype(jnp.int32)

    return lax.fori_loop(0, lon, scan, 0, unroll=4)


def toom_cook():
    pairs = [Fraction(1), Fraction(2), Fraction(1, 2), Fraction(3, 4)]
    squares = [p * p for p in pairs]

    def times(poly, root):
        low = [-root * v for v in poly] + [Fraction(0)]
        high = [Fraction(0)] + list(poly)
        return [p + q for p, q in zip(low, high)]

    def product(roots):
        poly = [Fraction(1)]
        for root in roots:
            poly = times(poly, root)
        return poly

    points = [Fraction(0)] + [v for p in pairs for v in (p, -p)]
    taps = []
    for p in points:
        scale = Fraction(1)
        for q in points:
            if q != p:
                scale = scale * (p - q)
        taps.append([float(p**i / scale) for i in range(7)])
    taps.append([0.0] * 6 + [1.0])
    inner = [[float(v) for v in product([q for q in squares if q != p])] for p in squares]
    whole = [float(v) for v in product(squares)]
    return [float(p) for p in pairs], taps, inner, whole


PAIRS, TAPS, INNER_POLY, WHOLE_POLY = toom_cook()
POINTS = len(TAPS)


def combine(values, coefs):
    total = None
    for v, c in zip(values, coefs):
        term = v if c == 1.0 else v * c
        total = term if total is None else total + term
    return total


def conv_blocks(blocks, wide, taps, bias):
    for m, d in enumerate(blocks):
        values = [combine(d[0:9:2], WHOLE_POLY)]
        for p, poly in zip(PAIRS, INNER_POLY):
            even = combine(d[2:9:2], poly)
            odd = combine(d[1:8:2], poly)
            if p != 1.0:
                odd = odd * p
            values += [even + odd, even - odd]
        values.append(combine(d[1:10:2], WHOLE_POLY))
        for n, v in enumerate(values):
            wide[m, n, pl.ds(0, 8), :] = v[16:]
            wide[m, n, pl.ds(8, 16), :] = v[:16]
            wide[m, n, pl.ds(24, 8), :] = v[16:]
    cells = [(m, h) for m in range(len(blocks)) for h in range(2)]

    def product(n):
        total = [None] * len(cells)
        for j in range(7):
            tap = taps[n * 7 + j]
            for i, (m, h) in enumerate(cells):
                term = wide[m, n, pl.ds(5 + j + 8 * h, 8), :] * tap
                total[i] = term if j == 0 else total[i] + term
        return total

    y = [[v + bias for v in product(0)]] + [[bias] * len(cells) for _ in range(3)]
    for q, p in enumerate(PAIRS):
        plus, minus = product(1 + 2 * q), product(2 + 2 * q)
        for i in range(len(cells)):
            s, t = plus[i] + minus[i], plus[i] - minus[i]
            y[0][i] = y[0][i] + s
            y[1][i] = y[1][i] + (t if p == 1.0 else t * p)
            y[2][i] = y[2][i] + (s if p == 1.0 else s * (p * p))
            y[3][i] = y[3][i] + (t if p == 1.0 else t * (p * p * p))
    last = product(POINTS - 1)
    y[3] = [v + w for v, w in zip(y[3], last)]
    return [[jnp.concatenate([y[r][2 * m], y[r][2 * m + 1]], axis=0) for r in range(4)]
            for m in range(len(blocks))]


def pointwise(conv, inp, gain, shift, w_in, b_in, w_out, b_out, scale):
    values = conv.astype(F32)
    centre = jnp.mean(values, axis=-1, keepdims=True)
    dev = values - centre
    spread = jnp.mean(dev * dev, axis=-1, keepdims=True)
    normed = (dev * lax.rsqrt(spread + 1e-06) * gain + shift).astype(BF16)
    h = jnp.dot(normed, w_in, preferred_element_type=F32) + b_in
    half = 0.5 * h
    hidden = (half + half * lax.erf(h * 0.7071067811865476)).astype(BF16)
    branch = jnp.dot(hidden, w_out, preferred_element_type=F32) + b_out
    return (inp.astype(F32) + scale * branch).astype(BF16)


def window_rows(src, rows, t, lon, keep):
    left = lax.rem(t + lon - 1, lon)
    right = lax.rem(t + 1, lon)
    keep_l, keep_c, keep_r = keep
    zero = jnp.zeros((), F32)
    first = lax.broadcasted_iota(jnp.int32, (8, C), 0) < 4
    keep_side = jnp.where(first, keep_r.astype(F32), keep_l.astype(F32)) > 0

    def tile(r, col):
        return src[r, pl.ds(pl.multiple_of(col * TS, TS), TS), :].astype(F32)

    out = []
    for r in rows:
        centre = tile(r, t)
        if keep_c is not None:
            centre = jnp.where(keep_c, centre, zero)
        side = jnp.where(first, tile(r, right)[:8], tile(r, left)[8:])
        out.append(jnp.concatenate([centre, jnp.where(keep_side, side, zero)], axis=0))
    return out


def neighbours(owner_ref, band, t, lon):
    left = lax.rem(t + lon - 1, lon)
    right = lax.rem(t + 1, lon)
    return (owner_ref[band, left] >= 0, owner_ref[band, t] >= 0, owner_ref[band, right] >= 0)


INNER, UPPER, LOWER, FULL = "inner_rows", "upper_rows", "lower_rows", "full_rows"
CELLS = {INNER: 128, UPPER: 64, LOWER: 64, FULL: 256}


def block_kernel(rows, want, batch, n_args, n_pass, *refs):
    args, refs = refs[:n_args], refs[n_args + n_pass :]
    send, refs = refs[0], refs[1:]
    held, refs = refs[:n_args], refs[n_args:]
    wide, taps, convbuf, inbuf, stage, seen, cols, dests, sem, load = refs
    loads = []
    for q, (src, dst) in enumerate(zip(args, held)):
        if rows in (UPPER, LOWER) and q == 1:
            part = src.at[pl.ds(0 if rows == UPPER else 9, 7)]
            loads.append(pltpu.make_async_copy(part, dst, load.at[q]))
        else:
            loads.append(pltpu.make_async_copy(src, dst, load.at[q]))
    for cp in loads:
        cp.start()
    owner_ref, x_ref = held[:2]
    top, bottom = held[2], held[-10]
    taps_in, bias_ref, gain, shift, w_in, b_in, w_out, b_out, scale = held[-9:]
    bands, lon = owner_ref.shape
    band = lax.axis_index("tile")
    loads[0].wait()
    count = list_wet(owner_ref, band, want, seen, cols, dests)
    loads[-9].wait()
    for j in range(7):
        column_taps = [
            jnp.broadcast_to(taps_in[i, pl.ds(j, 1), :].astype(F32), (8, C)) for i in range(7)]
        for n in range(POINTS):
            used = [(k, c) for k, c in zip(column_taps, TAPS[n]) if c != 0.0]
            total = combine(*zip(*used))
            taps[n * 7 + j] = total
    for cp in loads[1:-9] + loads[-8:]:
        cp.wait()
    cells = convbuf.shape[1]

    def copies(dest, q, b):
        def piece(p, lo, n, lev):
            return pltpu.make_async_copy(
                stage.at[b, q, pl.ds(lo, n)], send.at[dest, pl.ds(lev, n)], sem.at[b, q, p])

        half = send.shape[1] // 2
        if rows == FULL:
            return [piece(0, 0, 2 * half, 0)]
        if rows == INNER:
            return [piece(0, 0, half, half // 2)]
        return [piece(0, 0, half // 2, 0 if rows == UPPER else half + half // 2)]

    def each_copy(k, b, act):
        for q in range(batch):
            index = k * batch + q

            @pl.when(index < count)
            def _():
                for cp in copies(dests[index], q, b):
                    act(cp)

    def convolve(k, q):
        t = cols[k * batch + q]
        own = neighbours(owner_ref, band, t, lon)
        own = (own[0], None, own[2])
        bias = jnp.broadcast_to(bias_ref[...], (8, C))
        column = pl.ds(pl.multiple_of(t * TS, TS), TS)

        def window(src, picked, keep=own):
            return window_rows(src, picked, t, lon, keep)

        def above(n):
            up = neighbours(owner_ref, jnp.maximum(band - 1, 0), t, lon)
            return window(top, range(3), up) + window(x_ref, range(n))

        def below(n):
            down = neighbours(owner_ref, jnp.minimum(band + 1, bands - 1), t, lon)
            last = x_ref.shape[0]
            return window(x_ref, range(last - n, last)) + window(bottom, range(3), down)

        def put(first, blocks):
            for n, block in enumerate(conv_blocks(blocks, wide, taps, bias)):
                for r, out in enumerate(block):
                    convbuf[q, pl.ds((first + n * 4 + r) * TS, TS)] = out.astype(BF16)

        if rows == INNER:
            cut = window(x_ref, range(1, 15))
            put(0, [cut[:10], cut[4:]])
            inbuf[q] = x_ref[pl.ds(4, 8), column, :].reshape(cells, C)
        elif rows == UPPER:
            put(0, [above(7)])
            inbuf[q] = x_ref[pl.ds(0, 4), column, :].reshape(cells, C)
        elif rows == LOWER:
            put(0, [below(7)])
            inbuf[q] = x_ref[pl.ds(3, 4), column, :].reshape(cells, C)
        else:
            cut = above(11)
            put(0, [cut[:10], cut[4:]])
            cut = below(11)
            put(8, [cut[:10], cut[4:]])
            inbuf[q] = x_ref[:, column, :].reshape(cells, C)

    def step(k, _):
        b = lax.rem(k, SLOTS)

        @pl.when(k >= SLOTS)
        def _():
            each_copy(k - SLOTS, b, lambda cp: cp.wait())

        def one(q, _):
            convolve(k, q)
            return 0

        lax.fori_loop(0, jnp.minimum(batch, count - k * batch), one, 0)
        tiles = 512 // cells
        for part in range(0, batch, tiles):
            piece = pl.ds(part, tiles)
            stage[b, piece] = pointwise(
                convbuf[piece].reshape(512, C), inbuf[piece].reshape(512, C), gain[...], shift[...],
                w_in[...], b_in[...], w_out[...], b_out[...], scale[...],
            ).reshape((tiles,) + stage.shape[2:])
        each_copy(k, b, lambda cp: cp.start())
        return 0

    batches = lax.div(count + batch - 1, batch)
    lax.fori_loop(0, batches, step, 0)
    for d in range(SLOTS, 0, -1):
        k = batches - d

        @pl.when(k >= 0)
        def _():
            each_copy(k, lax.rem(k, SLOTS), lambda cp: cp.wait())


def block_call(rows, want, batch, owner, x, halos, consts, levels, alias=None, after=None):
    bands, lon = owner.shape
    hbm = pl.BlockSpec(memory_space=pltpu.HBM)
    args = [owner, x, *halos, *consts]
    n_args = len(args)
    held = [pltpu.SMEM(owner.shape, owner.dtype)]
    held.append(pltpu.VMEM((7 if rows in (UPPER, LOWER) else x.shape[0],) + x.shape[1:], x.dtype))
    held += [pltpu.VMEM(v.shape, v.dtype) for v in args[2:]]
    passed = [v for v in (alias, after) if v is not None]
    cells = CELLS[rows]
    share = TS * TS // levels
    return pl.pallas_call(
        functools.partial(block_kernel, rows, want, batch, n_args, len(passed)),
        in_specs=[hbm] * (n_args + len(passed)),
        out_specs=hbm,
        out_shape=jax.ShapeDtypeStruct((bands, levels, share, C), BF16),
        scratch_shapes=held + [
            pltpu.VMEM((2, POINTS, 32, C), F32),
            pltpu.VMEM((POINTS * 7, 8, C), F32),
            pltpu.VMEM((batch, cells, C), BF16),
            pltpu.VMEM((batch, cells, C), BF16),
            pltpu.VMEM((SLOTS, batch, cells // share, share, C), BF16),
            pltpu.SMEM((bands,), jnp.int32),
            pltpu.SMEM((lon + 1,), jnp.int32),
            pltpu.SMEM((lon + 1,), jnp.int32),
            pltpu.SemaphoreType.DMA((SLOTS, batch, 2)),
            pltpu.SemaphoreType.DMA((n_args + 1,)),
        ],
        input_output_aliases={} if alias is None else {n_args: 0},
        compiler_params=pltpu.CompilerParams(vmem_limit_bytes=VMEM_BYTES),
        cost_estimate=pl.CostEstimate(
            flops=bands * cells * C * (2 * 49 + 4 * 512) * 8, transcendentals=bands * cells * 512,
            bytes_accessed=2 * x.size + bands * cells * C * 2),
        name=rows,
    )(*args, *passed)


GROUP = 8


def vertical_kernel(src, rank, recv0, recv1, w_hbm, out, held, done, taps, w, sem_in,
                    sem_out, sem_w):
    tiles, levels, cells = held.shape[:3]

    def each_fetch(t, act):
        for r, recv in enumerate((recv0, recv1)):
            @pl.when(rank[t] == r)
            def _():
                act(pltpu.make_async_copy(recv.at[src[t]], held.at[t], sem_in.at[t]))

    def store(t):
        return pltpu.make_async_copy(done.at[t], out.at[t], sem_out.at[t])

    def start(t, _):
        each_fetch(t, lambda cp: cp.start())
        return 0

    weights = pltpu.make_async_copy(w_hbm, taps, sem_w)
    weights.start()
    lax.fori_loop(0, tiles, start, 0, unroll=8)
    weights.wait()
    for d in range(6):
        for p in range(2):
            k = d - p
            block = taps[k] if 0 <= k < 5 else jnp.zeros((C, C), BF16)
            w[pl.ds(d * C, C), pl.ds(p * C, C)] = block

    def step(g, _):
        for q in range(GROUP):
            each_fetch(g * GROUP + q, lambda cp: cp.wait())
        zero = jnp.zeros((cells, C), BF16)
        wide = []
        for q in range(GROUP):
            x = [zero, zero] + [held[g * GROUP + q, lev] for lev in range(levels)] + [zero, zero]
            wide += [jnp.concatenate(x[lev : lev + 6], axis=1) for lev in range(0, levels, 2)]
        total = jnp.dot(jnp.concatenate(wide, axis=0), w[...], preferred_element_type=F32)
        for q in range(GROUP):
            t = g * GROUP + q
            for lev in range(levels):
                row = (q * levels // 2 + lev // 2) * cells
                part = total[row : row + cells, (lev % 2) * C : (lev % 2 + 1) * C]
                done[t, lev] = (held[t, lev].astype(F32) + part).astype(BF16)
            store(t).start()
        return 0

    lax.fori_loop(0, tiles // GROUP, step, 0)

    def drain(t, _):
        store(t).wait()
        return 0

    lax.fori_loop(0, tiles, drain, 0)


def vertical_call(src, rank, recv0, recv1, w_vert):
    tiles = src.shape[0]
    levels, cells = recv0.shape[1:3]
    smem = pl.BlockSpec(memory_space=pltpu.SMEM)
    hbm = pl.BlockSpec(memory_space=pltpu.HBM)
    return pl.pallas_call(
        vertical_kernel,
        in_specs=[smem, smem, hbm, hbm, hbm],
        out_specs=hbm,
        out_shape=jax.ShapeDtypeStruct((tiles, levels, cells, C), BF16),
        scratch_shapes=[
            pltpu.VMEM((tiles, levels, cells, C), BF16),
            pltpu.VMEM((tiles, levels, cells, C), BF16),
            pltpu.VMEM((5, C, C), BF16),
            pltpu.VMEM((6 * C, 2 * C), BF16),
            pltpu.SemaphoreType.DMA((tiles,)),
            pltpu.SemaphoreType.DMA((tiles,)),
            pltpu.SemaphoreType.DMA,
        ],
        compiler_params=pltpu.CompilerParams(vmem_limit_bytes=VMEM_BYTES),
        name="vertical",
    )(src, rank, recv0, recv1, w_vert)


def halo_kernel(x, first, last, held, sem):
    rows = first.shape[0]
    ends = [(0, first), (x.shape[0] - rows, last)]
    loads = [pltpu.make_async_copy(x.at[pl.ds(row, rows)], held.at[q], sem.at[q])
             for q, (row, _) in enumerate(ends)]
    stores = [pltpu.make_async_copy(held.at[q], out, sem.at[2 + q])
              for q, (_, out) in enumerate(ends)]
    for cp in loads:
        cp.start()
    for load, store in zip(loads, stores):
        load.wait()
        store.start()
    for cp in stores:
        cp.wait()


def halo_call(x, rows):
    hbm = pl.BlockSpec(memory_space=pltpu.HBM)
    shape = jax.ShapeDtypeStruct((rows,) + x.shape[1:], x.dtype)
    return pl.pallas_call(
        halo_kernel,
        in_specs=[hbm],
        out_specs=[hbm] * 2,
        out_shape=[shape] * 2,
        scratch_shapes=[pltpu.VMEM((2, rows) + x.shape[1:], x.dtype), pltpu.SemaphoreType.DMA((4,))],
        compiler_params=pltpu.CompilerParams(vmem_limit_bytes=VMEM_BYTES),
        name="halo_rows",
    )(x)


def body(ocean_state, tile_owner, kernel, bias_dw, ln_gain, ln_bias, w_in, b_in, w_out, b_out,
         layer_scale, w_vert):
    bands, lon = tile_owner.shape
    levels = lax.axis_size("lev")
    band = lax.axis_index("tile")
    x = ocean_state[0]
    ends = bands - 1
    head, tail = halo_call(x, 3)
    top = lax.ppermute(tail, "tile", [(i, i + 1) for i in range(ends)])
    bottom = lax.ppermute(head, "tile", [(i + 1, i) for i in range(ends)])
    row = lambda v: v.reshape(1, -1)
    consts = (kernel, row(bias_dw), row(ln_gain), row(ln_bias), w_in, row(b_in), w_out, row(b_out),
              row(layer_scale))
    halos = (top, bottom)

    def exchange(sent):
        return lax.all_to_all(
            sent.reshape((bands * levels,) + sent.shape[2:]), ("tile", "lev"), split_axis=0,
            concat_axis=0, tiled=True,
        ).reshape(sent.shape)

    sent1 = block_call(INNER, 1, 4, tile_owner, x, (), consts, levels)
    sent1 = block_call(UPPER, 1, 8, tile_owner, x, (top,), consts, levels, alias=sent1)
    sent1 = block_call(LOWER, 1, 8, tile_owner, x, (bottom,), consts, levels, alias=sent1)
    sent0 = block_call(FULL, 0, 4, tile_owner, x, halos, consts, levels, after=sent1)
    sent0, recv1 = lax.optimization_barrier((sent0, exchange(sent1)))
    recv0 = exchange(sent0)

    owner_of = jnp.where(tile_owner >= 0, tile_owner // bands, -1)
    mine = owner_of == band
    before = jnp.cumsum(mine.astype(jnp.int32), axis=1) - mine
    hit = (tile_owner.reshape(1, -1) == (band * bands + jnp.arange(bands))[:, None])
    code = jnp.arange(bands, dtype=jnp.int32)[:, None] * CAP + before
    found = jnp.sum(jnp.where(hit, code.reshape(1, -1), 0), axis=1)
    return vertical_call(found // CAP, found % CAP, recv0, recv1, w_vert)


def solution(mesh):
    return jax.shard_map(
        body,
        mesh=mesh,
        in_specs=(P("lev", "tile", None, None),) + (P(),) * 11,
        out_specs=P("tile", None, "lev", None),
        check_vma=False,
    )
```
